32 devices in a mesh: groups: 1, seq: 16 (over z, y, x), section: 1, head: 2 (over core).
Axes of the slice: x: 2, y: 2, z: 4, core: 2. Of those that a mesh axis runs over, the one named last changes fastest.
Arguments:
- queries: bfloat16 [2560, 3072], P(('groups', 'seq', 'head'), 'section'), may hold values from -24 to 24
- keys: bfloat16 [2560, 3072], P(('groups', 'seq', 'head'), 'section'), may hold values from -10.5 to 10.5
- values: bfloat16 [2560, 3072], P(('groups', 'seq', 'head'), 'section'), may hold values from -6 to 6
- text_keys: bfloat16 [128, 3072], P(('groups', 'seq', 'head'), 'section'), may hold values from -10 to 10
- text_values: bfloat16 [128, 3072], P(('groups', 'seq', 'head'), 'section'), may hold values from -6 to 6
- text_length: int32 [1], P('groups'), may hold values from 32 to 128
- out_weight: bfloat16 [3072, 3072], P(None, 'section'), may hold values from -0.109375 to 0.109375
Outputs:
- projected: bfloat16 [2560, 3072], P(('groups', 'seq', 'head'), 'section')
The draws below stay inside these ranges and needn't reach their ends.
All inputs are finite; a program needn't handle non-finite values.
Results may differ from the reference program's by a relative error of at most 0.0065.
Values may be sent and summed in bfloat16 or wider, within the bound.
A program may use at most 128 MiB of HBM per device.

```python
import jax
import jax.numpy as jnp
from jax import lax

HEADS = 24
HEAD_DIM = 128
D = 3072
TXT = 128
TOKENS = 2560


spread = 1.7


def paired_draw(key):
    base = jax.random.fold_in(key, 41)
    query_key, keys_key = jax.random.split(base)
    query_draw = spread * jax.random.truncated_normal(query_key, -6.0, 6.0, (TOKENS, D), jnp.float32)
    keys_draw = spread * jax.random.truncated_normal(keys_key, -6.0, 6.0, (TOKENS, D), jnp.float32)
    return (query_draw, keys_draw)


def draw_queries(key, part):
    return paired_draw(key)[0].astype(jnp.bfloat16)


def draw_keys(key, part):
    return paired_draw(key)[1].astype(jnp.bfloat16)


def level_of(own_key, dims, pieces, least, high):
    def one(dim, blocks):
        steps = jax.random.uniform(jax.random.fold_in(jax.random.fold_in(own_key, 6), dim), (blocks,), jnp.float32, least / len(pieces), high / len(pieces))
        return jnp.repeat(jnp.exp(steps), dims[dim] // blocks).reshape((-1,) + (1,) * (len(dims) - dim - 1))

    factor_of = one(*pieces[0])
    for cut in pieces[1:]:
        factor_of = factor_of * one(*cut)
    return factor_of


def scatter_about(stream_key, dims, scale, limit, cuts=(), kind=jnp.bfloat16):
    array = jax.random.normal(stream_key, dims, jnp.float32) * scale
    if len(cuts) > 0:
        array = level_of(stream_key, dims, cuts, -0.22, 0.18) * array
    return jnp.clip(array, min=-limit, max=limit).astype(kind)


def setup_inputs(seed: int = 0, part: int = 0) -> dict:
    seeds = jax.random.split(jax.random.key(seed), 8)
    own_keys = jax.random.split(jax.random.fold_in(seeds[7], part), 8)
    queries = draw_queries(jax.random.fold_in(jax.random.fold_in(seeds[7], part), 71), part)
    keys = draw_keys(jax.random.fold_in(jax.random.fold_in(seeds[7], part), 71), part)
    values = scatter_about(own_keys[2], (TOKENS, D), 1.0, 6.0, ((0, 32),))
    text_keys = scatter_about(own_keys[3], (TXT, D), 1.7, 10.0, ((0, 32),))
    text_values = scatter_about(own_keys[4], (TXT, D), 1.0, 6.0, ((0, 32),))
    text_length = jax.random.randint(own_keys[5], (1,), TXT // 4, TXT + 1).astype(jnp.int32)
    out_weight = scatter_about(seeds[6], (D, D), D ** -0.5, 0.109375)
    return dict(queries=queries, keys=keys, values=values, text_keys=text_keys, text_values=text_values, text_length=text_length, out_weight=out_weight)


def reference(queries, keys, values, text_keys, text_values, text_length, out_weight):
    all_keys = jnp.concatenate([text_keys, keys], axis=0)
    all_values = jnp.concatenate([text_values, values], axis=0)
    usable = jnp.concatenate([jnp.arange(TXT) < text_length[0], jnp.ones((TOKENS,), dtype=bool)])
    queries_heads = queries.reshape(TOKENS, HEADS, HEAD_DIM).transpose(1, 0, 2)
    keys_heads = all_keys.reshape(TXT + TOKENS, HEADS, HEAD_DIM).transpose(1, 0, 2)
    values_heads = all_values.reshape(TXT + TOKENS, HEADS, HEAD_DIM).transpose(1, 0, 2)

    def one_head(operands):
        query_rows, key_rows, value_rows = operands
        scores = jnp.dot(query_rows, key_rows.T, preferred_element_type=jnp.float32) * (HEAD_DIM ** -0.5)
        scores = jnp.where(usable[None, :], scores, -1e30)
        highest = jnp.max(scores, axis=-1, keepdims=True)
        weights = jnp.exp(scores - highest)
        totals = jnp.sum(weights, axis=-1, keepdims=True)
        summed = jnp.dot(weights.astype(jnp.bfloat16), value_rows, preferred_element_type=jnp.float32)
        return summed / totals

    outputs = lax.map(one_head, (queries_heads, keys_heads, values_heads))
    attended = outputs.transpose(1, 0, 2).reshape(TOKENS, D).astype(jnp.bfloat16)
    return jnp.dot(attended, out_weight, preferred_element_type=jnp.float32).astype(jnp.bfloat16)
```

```python
import functools
import math

import jax
import jax.numpy as jnp
import numpy as np
from jax import lax
from jax.experimental import pallas as pl
from jax.experimental.pallas import tpu as pltpu
from jax.sharding import PartitionSpec as P

HEAD_DIM = 128
MESH = pl.DeviceIdType.MESH


def kernel(
    dims,
    length_ref,
    q_ref,
    k_ref,
    v_ref,
    tk_ref,
    tv_ref,
    order_ref,
    pick_hbm,
    w_hbm,
    o_ref,
    qb,
    kv,
    tb,
    tkv,
    ob,
    att,
    wb,
    acc,
    pick_ref,
    scores,
    wide,
    packed,
    t_ref,
    local_sem,
    w_sem,
    x_send,
    x_recv,
    t_send,
    t_recv,
    o_send,
    o_recv,
    kv2_send,
    kv2_recv,
    t2_send,
    t2_recv,
    entry,
):
    A, R, C, X, hp, Y, H, group = dims
    d = HEAD_DIM
    rows = q_ref.shape[0]
    Z, HB, G = A // Y, A // H, A // group
    seq = lax.axis_index("seq")
    core = lax.axis_index("head")
    section = lax.axis_index("section")
    a = seq // R
    r = lax.rem(seq, R)
    z, y = a // Y, lax.rem(a, Y)
    slot = r * C + core
    width = hp * d
    own_half = a // HB
    halves = [lax.rem(own_half + h, H) for h in range(H)]

    def at(a2=None, r2=None, c2=None, x2=None):
        return {
            "seq": (a if a2 is None else a2) * R + (r if r2 is None else r2),
            "head": core if c2 is None else c2,
            "section": section if x2 is None else x2,
        }

    def cols(start, size):
        return pl.ds(pl.multiple_of(start, d), size)

    def own_rows(which):
        return pl.ds(pl.multiple_of(which * rows, 16), rows)

    def half_rows(h):
        return pl.ds(pl.multiple_of(h * HB * rows, 16), HB * rows)

    def at_hops(k):
        for dy in range(min(Y - 1, k) + 1):
            dz = k - dy
            y2 = lax.rem(y + dy, Y)
            if dz == 0:
                yield None, z * Y + y2
            elif dz < Z:
                yield z + dz < Z, (z + dz) * Y + y2
                yield z - dz >= 0, (z - dz) * Y + y2

    def each(k, act):
        for there, a2 in at_hops(k):
            if there is None:
                act(a2)
            else:
                pl.when(there)(functools.partial(act, a2))

    hops = Z - 1 + Y - 1
    beside = (z > 0).astype(jnp.int32) + (z < Z - 1).astype(jnp.int32) + Y - 1
    barrier = pltpu.get_barrier_semaphore()

    def greet(target, sem=barrier):
        pl.semaphore_signal(sem, inc=1, device_id=target, device_id_type=MESH)

    staged = False
    if staged:
        each(1, lambda a2: greet(at(a2=a2)))
    else:
        for da in range(A):
            for dx in range(X):
                if da or dx:
                    greet(at(a2=lax.rem(a + da, A), x2=lax.rem(section + dx, X)))
    for dr in range(1, R):
        greet(at(r2=lax.rem(r + dr, R)))
    for dc in range(1, C):
        greet(at(c2=lax.rem(core + dc, C)))

    def remote(src, dst, send, recv, target):
        return pltpu.make_async_remote_copy(
            src_ref=src, dst_ref=dst, send_sem=send, recv_sem=recv, device_id=target, device_id_type=MESH
        )

    def drain(ref, sem):
        pltpu.make_async_copy(ref, ref, sem).wait()

    def landing(j, n):
        return qb.at[j] if n == 2 else kv.at[j, n, slot]

    def first(j, n, a2):
        src = (k_ref, v_ref, q_ref)[n].at[:, cols((a2 * hp + j) * d, d)]
        remote(src, landing(j, n).at[own_rows(a)], x_send, x_recv.at[j, n, own_half], at(a2=a2)).start()

    def first_own(j, n):
        src = (k_ref, v_ref, q_ref)[n].at[:, cols((a * hp + j) * d, d)]
        pltpu.make_async_copy(src, landing(j, n).at[own_rows(a)], x_recv.at[j, n, own_half]).start()

    def first_text(a2):
        remote(t_ref.at[:, cols(a2 * width, width)], tb.at[slot, a], t_send, t_recv, at(a2=a2)).start()

    count = tk_ref.shape[0]
    if 2 * count < wide.shape[0]:
        wide[...] = jnp.zeros_like(wide)
    wide[:count] = tk_ref[...].astype(jnp.float32)
    wide[count : 2 * count] = tv_ref[...].astype(jnp.float32)
    packed[...] = wide[...].astype(jnp.bfloat16)
    text_copy = pltpu.make_async_copy(packed, t_ref, local_sem)
    text_copy.start()
    for n in range(3):
        first_own(0, n)

    if staged:
        pl.semaphore_wait(barrier, beside + R - 1 + C - 1)
    else:
        pl.semaphore_wait(barrier, A * X - 1 + R - 1 + C - 1)
    for k in range(1, hops + 1):
        if staged and k > 1:
            pl.semaphore_wait(entry.at[k - 2], beside)
        if staged and k < hops:
            each(1, lambda a2: greet(at(a2=a2), entry.at[k - 1]))

    def send_all(j, which):
        for n in which:
            for da in range(1, A):
                first(j, n, lax.rem(a + da, A))
            if j > 0:
                first_own(j, n)

    text_copy.wait()
    pltpu.make_async_copy(t_ref.at[:, cols(a * width, width)], tb.at[slot, a], t_recv).start()
    for da in range(1, A):
        first_text(lax.rem(a + da, A))

    send_all(0, (0, 1))
    for j in range(hp):
        if j + 1 < hp:
            send_all(j + 1, (0, 1))
        send_all(j, (2,))

    pick_copy = pltpu.make_async_copy(pick_hbm, pick_ref, local_sem)
    pick_copy.start()
    for j in range(hp):
        for b in range(X * A):
            pltpu.make_async_copy(
                w_hbm.at[pl.ds((b * hp + j) * d, d)], wb.at[j, pl.ds(b * d, d)], w_sem.at[j]
            ).start()

    def members():
        for dr in range(1, R):
            yield dr - 1, at(r2=lax.rem(r + dr, R))
        for dc in range(1, C):
            yield R - 2 + dc, at(c2=lax.rem(core + dc, C))

    def share(block, send, recv):
        for n, target in members():
            remote(block(slot), block(slot), send, recv.at[n], target).start()

    def forward(block, send, recv):
        base = R - 1 + C - 1
        for dr in range(1, R):
            from_slot = lax.rem(r - dr + R, R) * C + core
            drain(block(from_slot), recv.at[dr - 1])
            for dc in range(1, C):
                n = base + (dr - 1) * (C - 1) + dc - 1
                remote(
                    block(from_slot), block(from_slot), send, recv.at[n], at(c2=lax.rem(core + dc, C))
                ).start()

    def collect(block, recv):
        base = R - 1 + C - 1
        for dc in range(1, C):
            from_core = lax.rem(core - dc + C, C)
            drain(block(r * C + from_core), recv.at[R - 2 + dc])
            for dr in range(1, R):
                n = base + (dr - 1) * (C - 1) + dc - 1
                drain(block(lax.rem(r - dr + R, R) * C + from_core), recv.at[n])

    def kv_block(j, n, h):
        return lambda s: kv.at[j, n, s, half_rows(h)]

    def text_block(s):
        return tb.at[s]

    def kv_sems(j, n, h):
        return kv2_send, kv2_recv.at[j, n, h]

    def share_kv(j, h):
        for n in range(2):
            drain(kv.at[j, n, slot, half_rows(h)], x_recv.at[j, n, h])
            share(kv_block(j, n, h), *kv_sems(j, n, h))

    def forward_kv(j, h):
        for n in range(2):
            forward(kv_block(j, n, h), *kv_sems(j, n, h))

    def collect_kv(j):
        for h in halves:
            for n in range(2):
                collect(kv_block(j, n, h), kv_sems(j, n, h)[1])

    def wait_q(j):
        for h in halves:
            drain(qb.at[j, half_rows(h)], x_recv.at[j, 2, h])

    def project(j, parts):
        for g in parts:
            drain(att.at[j, :, pl.ds(0, X * group * d)], o_recv.at[j, g])
        columns = o_ref.shape[1]
        step = 768 if columns % 768 == 0 else d
        if len(parts) == G:
            pieces = [pl.ds(0, X * A * d)]
        else:
            pieces = [cols((x * A + g * group) * d, group * d) for g in parts for x in range(X)]

        def run(first_term, last_term):
            @pl.loop(0, columns // step)
            def _(i):
                part = pl.ds(pl.multiple_of(i * step, d), step)
                term = None if first_term else acc[:, part]
                for piece in pieces:
                    got = jnp.dot(att[j, :, piece], wb[j, piece, part], preferred_element_type=jnp.float32)
                    term = got if term is None else term + got
                if last_term:
                    o_ref[:, part] = term.astype(o_ref.dtype)
                else:
                    acc[:, part] = term

        return run

    scale = math.log2(math.e) * d ** (-0.5)
    nt = (((1,), (1,)), ((), ()))
    total_keys = R * C * A * rows
    span = next((n for n in (640, 512, 256, 128) if total_keys % n == 0), total_keys)

    def lanes(x, combine, start):
        for c in range(0, x.shape[1], d):
            start = combine(start, x[:, c : c + d])
        return start

    def flat(j, n, s):
        return kv[j, n].reshape(-1, d)[s * span : (s + 1) * span]

    def attend(j):
        q = qb[j]
        text_scores = lax.dot_general(q, tkv[j, 0], nt, preferred_element_type=jnp.float32)
        text_scores = jnp.where(order_ref[...] < length_ref[0], text_scores, -1e30)
        top = lanes(text_scores[:, d:], jnp.maximum, text_scores[:, :d])
        for s in range(total_keys // span):
            part = lax.dot_general(q, flat(j, 0, s), nt, preferred_element_type=jnp.float32)
            scores[:, s * span : (s + 1) * span] = part
            top = lanes(part, jnp.maximum, top)
        top = jnp.max(top, axis=1, keepdims=True)
        p = jnp.exp2((text_scores - top) * scale)
        total = lanes(p[:, d:], jnp.add, p[:, :d])
        o = jnp.dot(p.astype(jnp.bfloat16), tkv[j, 1], preferred_element_type=jnp.float32)
        for s in range(total_keys // span):
            p = jnp.exp2((scores[:, s * span : (s + 1) * span] - top) * scale)
            total = lanes(p, jnp.add, total)
            o = o + jnp.dot(p.astype(jnp.bfloat16), flat(j, 1, s), preferred_element_type=jnp.float32)
        total = jnp.sum(total, axis=1, keepdims=True)
        ob[j] = (o / total).astype(jnp.bfloat16)

    column = cols((section * A + a) * d, d)
    own = a // group

    def back(j, a2, dx):
        remote(
            ob.at[j, own_rows(a2)],
            att.at[j, :, column],
            o_send,
            o_recv.at[j, own],
            at(a2=a2, x2=lax.rem(section + dx, X)),
        ).start()

    def back_group(j, i):
        for b in range(group):
            a2 = i * group + b
            for dx in range(1, X):
                back(j, a2, dx)

            @pl.when(a2 != a)
            def _():
                back(j, a2, 0)

            @pl.when(a2 == a)
            def _():
                pltpu.make_async_copy(ob.at[j, own_rows(a2)], att.at[j, :, column], o_recv.at[j, own]).start()

    def tile_at(k):
        if G & (G - 1):
            return lax.rem(own + 1 + k, G)
        across = jnp.where(own < G // 2, G - 1 - k, k)
        return jnp.where(k < G // 2, across, own ^ (G - 1 - k))

    def part_at(k):
        return lax.rem(own + k, G) if G & (G - 1) else own ^ k

    def attention(j):
        attend(j)

        @pl.loop(0, G)
        def _(k):
            back_group(j, tile_at(k))

    drain(tb.at[slot], t_recv)
    share(text_block, t2_send, t2_recv)
    for h in halves:
        share_kv(0, h)
    forward(text_block, t2_send, t2_recv)
    if hp > 1:
        for h in halves:
            share_kv(1, h)
    for h in halves:
        forward_kv(0, h)
    collect(text_block, t2_recv)
    pick_copy.wait()
    block = tb[...].reshape(-1, width)
    for n in range(2):
        got = jnp.dot(pick_ref[n], block, preferred_element_type=jnp.float32).astype(jnp.bfloat16)
        for i in range(hp):
            tkv[i, n] = got[:, i * d : (i + 1) * d]
    for j in range(hp):
        wait_q(j)
        collect_kv(j)
        attention(j)
        if j + 1 < hp:
            for h in halves:
                forward_kv(j + 1, h)
        if j + 2 < hp:
            for h in halves:
                share_kv(j + 2, h)
    for j in range(hp - 1):
        drain(wb.at[j], w_sem.at[j])
        project(j, list(range(G)))(j == 0, False)
    drain(wb.at[hp - 1], w_sem.at[hp - 1])
    others = R * C - 1
    if others:
        drain(kv.at[:, :, pl.ds(0, others)], kv2_send)
        drain(tb.at[pl.ds(0, others)], t2_send)
    if A > 1:
        for n in range(3):
            drain(qb.at[:, pl.ds(0, (A - 1) * rows)], x_send)
        drain(tb.at[slot, pl.ds(0, A - 1)], t_send)
    if G % 2:
        project(hp - 1, list(range(G)))(hp == 1, True)
    else:
        project(hp - 1, [part_at(k) for k in range(G // 2)])(hp == 1, False)
        project(hp - 1, [part_at(k) for k in range(G // 2, G)])(False, True)
    if A * X > 1:
        drain(att.at[:, :, pl.ds(0, (A * X - 1) * d)], o_send)


def shards(sizes, queries, keys, values, text_keys, text_values, text_length, out_weight):
    S, C, X = sizes
    rows, columns = queries.shape
    heads = columns // HEAD_DIM
    A = math.gcd(heads, S)
    R = S // A
    hp = heads // A
    text_rows = text_keys.shape[0]
    text = text_rows * S * C
    bf16 = jnp.bfloat16
    pad = -(-2 * text_rows // 8) * 8
    t = np.arange(text)
    block, i = t // text_rows, t % text_rows
    from_slot, from_a = block // A, block % A
    from_r, from_c = from_slot // C, from_slot % C
    order = (((from_a * R + from_r) * C + from_c) * text_rows + i).astype(np.int32)[None, :]
    pick = np.zeros((2, text, R * C * A * pad), np.float32)
    for n in range(2):
        pick[n, t, block * pad + n * text_rows + i] = 1.0
    pick = jnp.asarray(pick, bf16)
    out_columns = out_weight.shape[1]
    shares = R - 1 + C - 1 + (R - 1) * (C - 1)
    Y = H = group = 2 if A % 2 == 0 else 1
    vmem = pl.BlockSpec(memory_space=pltpu.VMEM)
    hbm = pl.BlockSpec(memory_space=pl.ANY)
    dma = pltpu.SemaphoreType.DMA
    return pl.pallas_call(
        functools.partial(kernel, (A, R, C, X, hp, Y, H, group)),
        out_shape=pltpu.VMEM((rows, out_columns), bf16),
        in_specs=[pl.BlockSpec(memory_space=pltpu.SMEM)] + [hbm] * 3 + [vmem] * 3 + [hbm] * 2,
        out_specs=vmem,
        scratch_shapes=[
            pltpu.VMEM((hp, A * rows, HEAD_DIM), bf16),
            pltpu.VMEM((hp, 2, R * C, A * rows, HEAD_DIM), bf16),
            pltpu.VMEM((R * C, A, pad, hp * HEAD_DIM), bf16),
            pltpu.VMEM((hp, 2, text, HEAD_DIM), bf16),
            pltpu.VMEM((hp, A * rows, HEAD_DIM), bf16),
            pltpu.VMEM((hp, rows, X * A * HEAD_DIM), bf16),
            pltpu.VMEM((hp, X * A * HEAD_DIM, out_columns), bf16),
            pltpu.VMEM((rows, out_columns), jnp.float32),
            pltpu.VMEM(pick.shape, bf16),
            pltpu.VMEM((A * rows, R * C * A * rows), jnp.float32),
            pltpu.VMEM((pad, columns), jnp.float32),
            pltpu.VMEM((pad, columns), bf16),
            pltpu.VMEM((pad, columns), bf16),
            dma,
            dma((hp,)),
            dma,
            dma((hp, 3, H)),
            dma,
            dma,
            dma,
            dma((hp, A // group)),
            dma,
            dma((hp, 2, H, shares)),
            dma,
            dma((shares,)),
            pltpu.SemaphoreType.REGULAR((A,)),
        ],
        compiler_params=pltpu.CompilerParams(
            collective_id=0, has_side_effects=True, vmem_limit_bytes=60 * 1024 * 1024
        ),
    )(text_length, queries, keys, values, text_keys, text_values, jnp.asarray(order), pick, out_weight)


def solution(mesh):
    sizes = (mesh.shape["seq"], mesh.shape["head"], mesh.shape["section"])
    tokens = P(("groups", "seq", "head"), "section")
    return jax.shard_map(
        functools.partial(shards, sizes),
        mesh=mesh,
        in_specs=(tokens,) * 5 + (P("groups"), P(None, "section")),
        out_specs=tokens,
        check_vma=False,
    )
```

```python
import functools
import math

import jax
import jax.numpy as jnp
import numpy as np
from jax import lax
from jax.experimental import pallas as pl
from jax.experimental.pallas import tpu as pltpu
from jax.sharding import PartitionSpec as P

HEAD_DIM = 128
MESH = pl.DeviceIdType.MESH


def kernel(
    dims,
    length_ref,
    q_ref,
    k_ref,
    v_ref,
    tk_hbm,
    tv_hbm,
    order_hbm,
    pick_hbm,
    w_hbm,
    o_ref,
    qb,
    kv,
    tb,
    tkv,
    ob,
    att,
    wb,
    acc,
    pick_ref,
    scores,
    tk_ref,
    tv_ref,
    order_ref,
    wide,
    packed,
    t_ref,
    local_sem,
    early_sem,
    w_sem,
    x_send,
    x_recv,
    t_send,
    t_recv,
    o_send,
    o_recv,
    kv2_send,
    kv2_recv,
    t2_send,
    t2_recv,
):
    A, R, C, X, hp, H, group = dims
    d = HEAD_DIM
    rows = q_ref.shape[0]
    HB, G = A // H, A // group
    seq = lax.axis_index("seq")
    core = lax.axis_index("head")
    section = lax.axis_index("section")
    a = seq // R
    r = lax.rem(seq, R)
    slot = r * C + core
    width = hp * d
    own_half = a // HB
    halves = [lax.rem(own_half + h, H) for h in range(H)]

    def at(a2=None, r2=None, c2=None, x2=None):
        return {
            "seq": (a if a2 is None else a2) * R + (r if r2 is None else r2),
            "head": core if c2 is None else c2,
            "section": section if x2 is None else x2,
        }

    def cols(start, size):
        return pl.ds(pl.multiple_of(start, d), size)

    def own_rows(which):
        return pl.ds(pl.multiple_of(which * rows, 16), rows)

    def half_rows(h):
        return pl.ds(pl.multiple_of(h * HB * rows, 16), HB * rows)

    barrier = pltpu.get_barrier_semaphore()

    def greet(target):
        pl.semaphore_signal(barrier, inc=1, device_id=target, device_id_type=MESH)

    for da in range(A):
        for dx in range(X):
            if da or dx:
                greet(at(a2=lax.rem(a + da, A), x2=lax.rem(section + dx, X)))
    for dr in range(1, R):
        greet(at(r2=lax.rem(r + dr, R)))
    for dc in range(1, C):
        greet(at(c2=lax.rem(core + dc, C)))

    def remote(src, dst, send, recv, target):
        return pltpu.make_async_remote_copy(
            src_ref=src, dst_ref=dst, send_sem=send, recv_sem=recv, device_id=target, device_id_type=MESH
        )

    def drain(ref, sem):
        pltpu.make_async_copy(ref, ref, sem).wait()

    def landing(j, n):
        return qb.at[j] if n == 2 else kv.at[j, n, slot]

    def first(j, n, a2):
        src = (k_ref, v_ref, q_ref)[n].at[:, cols((a2 * hp + j) * d, d)]
        remote(src, landing(j, n).at[own_rows(a)], x_send, x_recv.at[j, H if n == 2 else own_half], at(a2=a2)).start()

    def first_own(j, n):
        src = (k_ref, v_ref, q_ref)[n].at[:, cols((a * hp + j) * d, d)]
        pltpu.make_async_copy(src, landing(j, n).at[own_rows(a)], x_recv.at[j, H if n == 2 else own_half]).start()

    def first_text(a2):
        remote(t_ref.at[:, cols(a2 * width, width)], tb.at[slot, a], t_send, t_recv, at(a2=a2)).start()

    staged = [(tk_hbm, tk_ref), (tv_hbm, tv_ref), (order_hbm, order_ref), (pick_hbm, pick_ref)]
    staged = [pltpu.make_async_copy(src, dst, early_sem.at[i]) for i, (src, dst) in enumerate(staged)]
    for copy in staged:
        copy.start()
    for copy in staged:
        copy.wait()
    count = tk_ref.shape[0]
    if 2 * count < wide.shape[0]:
        wide[...] = jnp.zeros_like(wide)
    wide[:count] = tk_ref[...].astype(jnp.float32)
    wide[count : 2 * count] = tv_ref[...].astype(jnp.float32)
    packed[...] = wide[...].astype(jnp.bfloat16)
    text_copy = pltpu.make_async_copy(packed, t_ref, local_sem)
    text_copy.start()
    for n in range(3):
        first_own(0, n)

    pl.semaphore_wait(barrier, A * X - 1 + R - 1 + C - 1)

    def send_all(j, which):
        for n in which:
            for da in range(1, A):
                first(j, n, lax.rem(a + da, A))
            if j > 0:
                first_own(j, n)

    text_copy.wait()
    pltpu.make_async_copy(t_ref.at[:, cols(a * width, width)], tb.at[slot, a], t_recv).start()
    for da in range(1, A):
        first_text(lax.rem(a + da, A))

    send_all(0, (0, 1))
    for j in range(hp):
        if j + 1 < hp:
            send_all(j + 1, (0, 1))
        send_all(j, (2,))

    for j in range(hp):
        for b in range(X * A):
            pltpu.make_async_copy(
                w_hbm.at[pl.ds((b * hp + j) * d, d)], wb.at[j, pl.ds(b * d, d)], w_sem
            ).start()

    def members():
        for dr in range(1, R):
            yield dr - 1, at(r2=lax.rem(r + dr, R))
        for dc in range(1, C):
            yield R - 2 + dc, at(c2=lax.rem(core + dc, C))

    def share(block, send, recv):
        for n, target in members():
            remote(block(slot), block(slot), send, recv.at[n], target).start()

    def forward(block, send, recv):
        base = R - 1 + C - 1
        for dr in range(1, R):
            from_slot = lax.rem(r - dr + R, R) * C + core
            drain(block(from_slot), recv.at[dr - 1])
            for dc in range(1, C):
                n = base + (dr - 1) * (C - 1) + dc - 1
                remote(
                    block(from_slot), block(from_slot), send, recv.at[n], at(c2=lax.rem(core + dc, C))
                ).start()

    def collect(block, recv):
        base = R - 1 + C - 1
        for dc in range(1, C):
            from_core = lax.rem(core - dc + C, C)
            drain(block(r * C + from_core), recv.at[R - 2 + dc])
            for dr in range(1, R):
                n = base + (dr - 1) * (C - 1) + dc - 1
                drain(block(lax.rem(r - dr + R, R) * C + from_core), recv.at[n])

    def kv_block(j, h):
        return lambda s: kv.at[j, :, s, half_rows(h)]

    def text_block(s):
        return tb.at[s]

    def share_kv(j, h):
        drain(kv.at[j, :, slot, half_rows(h)], x_recv.at[j, h])
        share(kv_block(j, h), kv2_send, kv2_recv.at[j, h])

    def forward_kv(j, h):
        forward(kv_block(j, h), kv2_send, kv2_recv.at[j, h])

    def collect_kv(j):
        for h in halves:
            collect(kv_block(j, h), kv2_recv.at[j, h])

    def wait_q(j):
        drain(qb.at[j], x_recv.at[j, H])

    def project(j, parts, first_term, last_term):
        columns = o_ref.shape[1]
        step = 768 if columns % 768 == 0 else d
        if parts is None:
            drain(att.at[j], o_recv.at[j])
            pieces = [pl.ds(0, X * A * d)]
        else:
            for h in parts:
                drain(att.at[j, :, pl.ds(0, X * HB * d)], o_recv.at[j + h])
            pieces = [cols((x * A + h * HB) * d, HB * d) for h in parts for x in range(X)]

        @pl.loop(0, columns // step)
        def _(i):
            part = pl.ds(pl.multiple_of(i * step, d), step)
            term = None if first_term else acc[:, part]
            for piece in pieces:
                got = jnp.dot(att[j, :, piece], wb[j, piece, part], preferred_element_type=jnp.float32)
                term = got if term is None else term + got
            if last_term:
                o_ref[:, part] = term.astype(o_ref.dtype)
            else:
                acc[:, part] = term

    scale = math.log2(math.e) * d ** (-0.5)
    nt = (((1,), (1,)), ((), ()))
    total_keys = R * C * A * rows
    span = next((n for n in (640, 512, 256, 128) if total_keys % n == 0), total_keys)

    def lanes(x, combine, start):
        for c in range(0, x.shape[1], d):
            start = combine(start, x[:, c : c + d])
        return start

    def flat(j, n, s):
        return kv[j, n].reshape(-1, d)[s * span : (s + 1) * span]

    def attend(j):
        q = qb[j]
        text_scores = lax.dot_general(q, tkv[j, 0], nt, preferred_element_type=jnp.float32)
        text_scores = jnp.where(order_ref[...] < length_ref[0], text_scores, -1e30)
        top = lanes(text_scores[:, d:], jnp.maximum, text_scores[:, :d])
        for s in range(total_keys // span):
            part = lax.dot_general(q, flat(j, 0, s), nt, preferred_element_type=jnp.float32)
            scores[:, s * span : (s + 1) * span] = part
            top = lanes(part, jnp.maximum, top)
        top = jnp.max(top, axis=1, keepdims=True)
        p = jnp.exp2((text_scores - top) * scale)
        total = lanes(p[:, d:], jnp.add, p[:, :d])
        o = jnp.dot(p.astype(jnp.bfloat16), tkv[j, 1], preferred_element_type=jnp.float32)
        for s in range(total_keys // span):
            p = jnp.exp2((scores[:, s * span : (s + 1) * span] - top) * scale)
            total = lanes(p, jnp.add, total)
            o = o + jnp.dot(p.astype(jnp.bfloat16), flat(j, 1, s), preferred_element_type=jnp.float32)
        total = jnp.sum(total, axis=1, keepdims=True)
        ob[j] = (o / total).astype(jnp.bfloat16)

    column = cols((section * A + a) * d, d)
    own = a // group

    def back(j, a2, dx):
        remote(
            ob.at[j, own_rows(a2)],
            att.at[j, :, column],
            o_send,
            o_recv.at[j + own_half if j == hp - 1 else j],
            at(a2=a2, x2=lax.rem(section + dx, X)),
        ).start()

    def back_group(j, i):
        for b in range(group):
            a2 = i * group + b
            for dx in range(1, X):
                back(j, a2, dx)

            @pl.when(a2 != a)
            def _():
                back(j, a2, 0)

            @pl.when(a2 == a)
            def _():
                pltpu.make_async_copy(ob.at[j, own_rows(a2)], att.at[j, :, column], o_recv.at[j + own_half if j == hp - 1 else j]).start()

    def tile_at(k):
        if G & (G - 1):
            return lax.rem(own + 1 + k, G)
        across = jnp.where(own < G // 2, G - 1 - k, k)
        return jnp.where(k < G // 2, across, own ^ (G - 1 - k))

    def attention(j):
        attend(j)

        @pl.loop(0, G)
        def _(k):
            back_group(j, tile_at(k))

    drain(tb.at[slot], t_recv)
    share(text_block, t2_send, t2_recv)
    for h in halves:
        share_kv(0, h)
    forward(text_block, t2_send, t2_recv)
    if hp > 1:
        for h in halves:
            share_kv(1, h)
    for h in halves:
        forward_kv(0, h)
    collect(text_block, t2_recv)
    block = tb[...].reshape(-1, width)
    for n in range(2):
        got = jnp.dot(pick_ref[n], block, preferred_element_type=jnp.float32).astype(jnp.bfloat16)
        for i in range(hp):
            tkv[i, n] = got[:, i * d : (i + 1) * d]
    for j in range(hp):
        wait_q(j)
        collect_kv(j)
        attention(j)
        if j + 1 < hp:
            for h in halves:
                forward_kv(j + 1, h)
        if j + 2 < hp:
            for h in halves:
                share_kv(j + 2, h)
    drain(wb, w_sem)
    for j in range(hp - 1):
        project(j, None, j == 0, False)
    others = R * C - 1
    if others:
        drain(kv.at[:, :, pl.ds(0, others)], kv2_send)
        drain(tb.at[pl.ds(0, others)], t2_send)
    if A > 1:
        for n in range(3):
            drain(qb.at[:, pl.ds(0, (A - 1) * rows)], x_send)
        drain(tb.at[slot, pl.ds(0, A - 1)], t_send)
    for k, h in enumerate(halves):
        project(hp - 1, [h], hp == 1 and k == 0, k == H - 1)
    if A * X > 1:
        drain(att.at[:, :, pl.ds(0, (A * X - 1) * d)], o_send)


def shards(sizes, queries, keys, values, text_keys, text_values, text_length, out_weight):
    S, C, X = sizes
    rows, columns = queries.shape
    heads = columns // HEAD_DIM
    A = math.gcd(heads, S)
    R = S // A
    hp = heads // A
    text_rows = text_keys.shape[0]
    text = text_rows * S * C
    bf16 = jnp.bfloat16
    pad = -(-2 * text_rows // 8) * 8
    t = np.arange(text)
    block, i = t // text_rows, t % text_rows
    from_slot, from_a = block // A, block % A
    from_r, from_c = from_slot // C, from_slot % C
    order = (((from_a * R + from_r) * C + from_c) * text_rows + i).astype(np.int32)[None, :]
    pick = np.zeros((2, text, R * C * A * pad), np.float32)
    for n in range(2):
        pick[n, t, block * pad + n * text_rows + i] = 1.0
    pick = jnp.asarray(pick, bf16)
    out_columns = out_weight.shape[1]
    shares = R - 1 + C - 1 + (R - 1) * (C - 1)
    H = group = 2 if A % 2 == 0 else 1
    vmem = pl.BlockSpec(memory_space=pltpu.VMEM)
    hbm = pl.BlockSpec(memory_space=pl.ANY)
    dma = pltpu.SemaphoreType.DMA
    return pl.pallas_call(
        functools.partial(kernel, (A, R, C, X, hp, H, group)),
        out_shape=pltpu.VMEM((rows, out_columns), bf16),
        in_specs=[pl.BlockSpec(memory_space=pltpu.SMEM)] + [hbm] * 8,
        out_specs=vmem,
        scratch_shapes=[
            pltpu.VMEM((hp, A * rows, HEAD_DIM), bf16),
            pltpu.VMEM((hp, 2, R * C, A * rows, HEAD_DIM), bf16),
            pltpu.VMEM((R * C, A, pad, hp * HEAD_DIM), bf16),
            pltpu.VMEM((hp, 2, text, HEAD_DIM), bf16),
            pltpu.VMEM((hp, A * rows, HEAD_DIM), bf16),
            pltpu.VMEM((hp, rows, X * A * HEAD_DIM), bf16),
            pltpu.VMEM((hp, X * A * HEAD_DIM, out_columns), bf16),
            pltpu.VMEM((rows, out_columns), jnp.float32),
            pltpu.VMEM(pick.shape, bf16),
            pltpu.VMEM((A * rows, R * C * A * rows), jnp.float32),
            pltpu.VMEM(text_keys.shape, bf16),
            pltpu.VMEM(text_values.shape, bf16),
            pltpu.VMEM((1, text), jnp.int32),
            pltpu.VMEM((pad, columns), jnp.float32),
            pltpu.VMEM((pad, columns), bf16),
            pltpu.VMEM((pad, columns), bf16),
            dma,
            dma((4,)),
            dma,
            dma,
            dma((hp, H + 1)),
            dma,
            dma,
            dma,
            dma((hp - 1 + H,)),
            dma,
            dma((hp, H, shares)),
            dma,
            dma((shares,)),
        ],
        compiler_params=pltpu.CompilerParams(
            collective_id=0, has_side_effects=True, vmem_limit_bytes=60 * 1024 * 1024
        ),
    )(text_length, queries, keys, values, text_keys, text_values, jnp.asarray(order), pick, out_weight)


def solution(mesh):
    sizes = (mesh.shape["seq"], mesh.shape["head"], mesh.shape["section"])
    tokens = P(("groups", "seq", "head"), "section")
    return jax.shard_map(
        functools.partial(shards, sizes),
        mesh=mesh,
        in_specs=(tokens,) * 5 + (P("groups"), P(None, "section")),
        out_specs=tokens,
        check_vma=False,
    )
```

```python
import functools
import math

import jax
import jax.numpy as jnp
import numpy as np
from jax import lax
from jax.experimental import pallas as pl
from jax.experimental.pallas import tpu as pltpu
from jax.sharding import PartitionSpec as P

HEAD_DIM = 128
MESH = pl.DeviceIdType.MESH


def kernel(
    dims,
    length_ref,
    q_ref,
    k_ref,
    v_ref,
    tk_hbm,
    tv_hbm,
    order_hbm,
    pick_hbm,
    w_hbm,
    o_ref,
    qb,
    kv,
    tb,
    tkv,
    ob,
    att,
    wb,
    acc,
    pick_ref,
    scores,
    tk_ref,
    tv_ref,
    order_ref,
    wide,
    packed,
    t_ref,
    local_sem,
    early_sem,
    w_sem,
    x_send,
    x_recv,
    t_send,
    t_recv,
    o_send,
    o_recv,
    kv2_send,
    kv2_recv,
    t2_send,
    t2_recv,
):
    A, R, C, X, hp, H, group = dims
    d = HEAD_DIM
    rows = q_ref.shape[0]
    HB, G = A // H, A // group
    seq = lax.axis_index("seq")
    core = lax.axis_index("head")
    section = lax.axis_index("section")
    a = seq // R
    r = lax.rem(seq, R)
    slot = r * C + core
    width = hp * d
    own_half = a // HB
    halves = [lax.rem(own_half + h, H) for h in range(H)]

    def at(a2=None, r2=None, c2=None, x2=None):
        return {
            "seq": (a if a2 is None else a2) * R + (r if r2 is None else r2),
            "head": core if c2 is None else c2,
            "section": section if x2 is None else x2,
        }

    def cols(start, size):
        return pl.ds(pl.multiple_of(start, d), size)

    def own_rows(which):
        return pl.ds(pl.multiple_of(which * rows, 16), rows)

    def half_rows(h):
        return pl.ds(pl.multiple_of(h * HB * rows, 16), HB * rows)

    barrier = pltpu.get_barrier_semaphore()

    def greet(target):
        pl.semaphore_signal(barrier, inc=1, device_id=target, device_id_type=MESH)

    for da in range(A):
        for dx in range(X):
            if da or dx:
                greet(at(a2=lax.rem(a + da, A), x2=lax.rem(section + dx, X)))
    for dr in range(1, R):
        greet(at(r2=lax.rem(r + dr, R)))
    for dc in range(1, C):
        greet(at(c2=lax.rem(core + dc, C)))

    def remote(src, dst, send, recv, target):
        return pltpu.make_async_remote_copy(
            src_ref=src, dst_ref=dst, send_sem=send, recv_sem=recv, device_id=target, device_id_type=MESH
        )

    def drain(ref, sem):
        pltpu.make_async_copy(ref, ref, sem).wait()

    def landing(j, n):
        return qb.at[j] if n == 2 else kv.at[j, n, slot]

    def first(j, n, a2):
        src = (k_ref, v_ref, q_ref)[n].at[:, cols((a2 * hp + j) * d, d)]
        remote(src, landing(j, n).at[own_rows(a)], x_send, x_recv.at[j, H if n == 2 else own_half], at(a2=a2)).start()

    def first_own(j, n):
        src = (k_ref, v_ref, q_ref)[n].at[:, cols((a * hp + j) * d, d)]
        pltpu.make_async_copy(src, landing(j, n).at[own_rows(a)], x_recv.at[j, H if n == 2 else own_half]).start()

    def first_text(a2):
        remote(t_ref.at[:, cols(a2 * width, width)], tb.at[slot, a], t_send, t_recv, at(a2=a2)).start()

    staged = [(tk_hbm, tk_ref), (tv_hbm, tv_ref), (order_hbm, order_ref), (pick_hbm, pick_ref)]
    staged = [pltpu.make_async_copy(src, dst, early_sem.at[i]) for i, (src, dst) in enumerate(staged)]
    for copy in staged:
        copy.start()
    for copy in staged:
        copy.wait()
    count = tk_ref.shape[0]
    if 2 * count < wide.shape[0]:
        wide[...] = jnp.zeros_like(wide)
    wide[:count] = tk_ref[...].astype(jnp.float32)
    wide[count : 2 * count] = tv_ref[...].astype(jnp.float32)
    packed[...] = wide[...].astype(jnp.bfloat16)
    text_copy = pltpu.make_async_copy(packed, t_ref, local_sem)
    text_copy.start()
    for n in range(3):
        first_own(0, n)

    pl.semaphore_wait(barrier, A * X - 1 + R - 1 + C - 1)

    def send_all(j, which):
        for n in which:
            for da in range(1, A):
                first(j, n, lax.rem(a + da, A))
            if j > 0:
                first_own(j, n)

    text_copy.wait()
    pltpu.make_async_copy(t_ref.at[:, cols(a * width, width)], tb.at[slot, a], t_recv).start()
    for da in range(1, A):
        first_text(lax.rem(a + da, A))

    send_all(0, (0, 1))
    for j in range(hp):
        if j + 1 < hp:
            send_all(j + 1, (0, 1))
        send_all(j, (2,))

    for j in range(hp):
        for b in range(X * A):
            pltpu.make_async_copy(
                w_hbm.at[pl.ds((b * hp + j) * d, d)], wb.at[j, pl.ds(b * d, d)], w_sem
            ).start()

    def members():
        for dr in range(1, R):
            yield dr - 1, at(r2=lax.rem(r + dr, R))
        for dc in range(1, C):
            yield R - 2 + dc, at(c2=lax.rem(core + dc, C))

    def share(block, send, recv):
        for n, target in members():
            remote(block(slot), block(slot), send, recv.at[n], target).start()

    def forward(block, send, recv):
        base = R - 1 + C - 1
        for dr in range(1, R):
            from_slot = lax.rem(r - dr + R, R) * C + core
            drain(block(from_slot), recv.at[dr - 1])
            for dc in range(1, C):
                n = base + (dr - 1) * (C - 1) + dc - 1
                remote(
                    block(from_slot), block(from_slot), send, recv.at[n], at(c2=lax.rem(core + dc, C))
                ).start()

    def collect(block, recv):
        base = R - 1 + C - 1
        for dc in range(1, C):
            from_core = lax.rem(core - dc + C, C)
            drain(block(r * C + from_core), recv.at[R - 2 + dc])
            for dr in range(1, R):
                n = base + (dr - 1) * (C - 1) + dc - 1
                drain(block(lax.rem(r - dr + R, R) * C + from_core), recv.at[n])

    def kv_block(j, h):
        return lambda s: kv.at[j, :, s, half_rows(h)]

    def text_block(s):
        return tb.at[s]

    def share_kv(j, h):
        drain(kv.at[j, :, slot, half_rows(h)], x_recv.at[j, h])
        share(kv_block(j, h), kv2_send, kv2_recv.at[j, h])

    def forward_kv(j, h):
        forward(kv_block(j, h), kv2_send, kv2_recv.at[j, h])

    def collect_kv(j):
        for h in halves:
            collect(kv_block(j, h), kv2_recv.at[j, h])

    def wait_q(j):
        drain(qb.at[j], x_recv.at[j, H])

    def project(j, parts, first_term, last_term):
        columns = o_ref.shape[1]
        step = 1536 if columns % 1536 == 0 else d
        if parts is None:
            drain(att.at[j], o_recv.at[j])
            pieces = [pl.ds(0, X * A * d)]
        else:
            for h in parts:
                drain(att.at[j, :, pl.ds(0, X * HB * d)], o_recv.at[j + h])
            pieces = [cols((x * A + h * HB) * d, HB * d) for h in parts for x in range(X)]

        @pl.loop(0, columns // step)
        def _(i):
            part = pl.ds(pl.multiple_of(i * step, d), step)
            term = None if first_term else acc[:, part]
            for piece in pieces:
                got = jnp.dot(att[j, :, piece], wb[j, piece, part], preferred_element_type=jnp.float32)
                term = got if term is None else term + got
            if last_term:
                o_ref[:, part] = term.astype(o_ref.dtype)
            else:
                acc[:, part] = term

    scale = math.log2(math.e) * d ** (-0.5)
    nt = (((1,), (1,)), ((), ()))
    total_keys = R * C * A * rows
    span = next((n for n in (640, 512, 256, 128) if total_keys % n == 0), total_keys)

    def lanes(x, combine, start):
        for c in range(0, x.shape[1], d):
            start = combine(start, x[:, c : c + d])
        return start

    def flat(j, n, s):
        return kv[j, n].reshape(-1, d)[s * span : (s + 1) * span]

    def attend(j):
        q = qb[j]
        text_scores = lax.dot_general(q, tkv[j, 0], nt, preferred_element_type=jnp.float32)
        text_scores = jnp.where(order_ref[...] < length_ref[0], text_scores, -1e30)
        top = lanes(text_scores[:, d:], jnp.maximum, text_scores[:, :d])
        for s in range(total_keys // span):
            part = lax.dot_general(q, flat(j, 0, s), nt, preferred_element_type=jnp.float32)
            scores[:, s * span : (s + 1) * span] = part
            top = lanes(part, jnp.maximum, top)
        top = jnp.max(top, axis=1, keepdims=True)
        p = jnp.exp2((text_scores - top) * scale)
        total = lanes(p[:, d:], jnp.add, p[:, :d])
        o = jnp.dot(p.astype(jnp.bfloat16), tkv[j, 1], preferred_element_type=jnp.float32)
        for s in range(total_keys // span):
            p = jnp.exp2((scores[:, s * span : (s + 1) * span] - top) * scale)
            total = lanes(p, jnp.add, total)
            o = o + jnp.dot(p.astype(jnp.bfloat16), flat(j, 1, s), preferred_element_type=jnp.float32)
        total = jnp.sum(total, axis=1, keepdims=True)
        ob[j] = (o / total).astype(jnp.bfloat16)

    column = cols((section * A + a) * d, d)
    own = a // group

    def back(j, a2, dx):
        remote(
            ob.at[j, own_rows(a2)],
            att.at[j, :, column],
            o_send,
            o_recv.at[j + own_half if j == hp - 1 else j],
            at(a2=a2, x2=lax.rem(section + dx, X)),
        ).start()

    def back_group(j, i):
        for b in range(group):
            a2 = i * group + b
            for dx in range(1, X):
                back(j, a2, dx)

            @pl.when(a2 != a)
            def _():
                back(j, a2, 0)

            @pl.when(a2 == a)
            def _():
                pltpu.make_async_copy(ob.at[j, own_rows(a2)], att.at[j, :, column], o_recv.at[j + own_half if j == hp - 1 else j]).start()

    def attention(j):
        attend(j)

        @pl.loop(0, G)
        def _(k):
            back_group(j, lax.rem(own + 1 + k, G))

    drain(tb.at[slot], t_recv)
    share(text_block, t2_send, t2_recv)
    for h in halves:
        share_kv(0, h)
    forward(text_block, t2_send, t2_recv)
    if hp > 1:
        for h in halves:
            share_kv(1, h)
    for h in halves:
        forward_kv(0, h)
    collect(text_block, t2_recv)
    block = tb[...].reshape(-1, width)
    for n in range(2):
        got = jnp.dot(pick_ref[n], block, preferred_element_type=jnp.float32).astype(jnp.bfloat16)
        for i in range(hp):
            tkv[i, n] = got[:, i * d : (i + 1) * d]
    for j in range(hp):
        wait_q(j)
        collect_kv(j)
        attention(j)
        if j + 1 < hp:
            for h in halves:
                forward_kv(j + 1, h)
        if j + 2 < hp:
            for h in halves:
                share_kv(j + 2, h)
    drain(wb, w_sem)
    for j in range(hp - 1):
        project(j, None, j == 0, False)
    others = R * C - 1
    if others:
        drain(kv.at[:, :, pl.ds(0, others)], kv2_send)
        drain(tb.at[pl.ds(0, others)], t2_send)
    if A > 1:
        for n in range(3):
            drain(qb.at[:, pl.ds(0, (A - 1) * rows)], x_send)
        drain(tb.at[slot, pl.ds(0, A - 1)], t_send)
    for k, h in enumerate(halves):
        project(hp - 1, [h], hp == 1 and k == 0, k == H - 1)
    if A * X > 1:
        drain(att.at[:, :, pl.ds(0, (A * X - 1) * d)], o_send)


def shards(sizes, queries, keys, values, text_keys, text_values, text_length, out_weight):
    S, C, X = sizes
    rows, columns = queries.shape
    heads = columns // HEAD_DIM
    A = math.gcd(heads, S)
    R = S // A
    hp = heads // A
    text_rows = text_keys.shape[0]
    text = text_rows * S * C
    bf16 = jnp.bfloat16
    pad = -(-2 * text_rows // 8) * 8
    t = np.arange(text)
    block, i = t // text_rows, t % text_rows
    from_slot, from_a = block // A, block % A
    from_r, from_c = from_slot // C, from_slot % C
    order = (((from_a * R + from_r) * C + from_c) * text_rows + i).astype(np.int32)[None, :]
    pick = np.zeros((2, text, R * C * A * pad), np.float32)
    for n in range(2):
        pick[n, t, block * pad + n * text_rows + i] = 1.0
    pick = jnp.asarray(pick, bf16)
    out_columns = out_weight.shape[1]
    shares = R - 1 + C - 1 + (R - 1) * (C - 1)
    H = group = 2 if A % 2 == 0 else 1
    vmem = pl.BlockSpec(memory_space=pltpu.VMEM)
    hbm = pl.BlockSpec(memory_space=pl.ANY)
    dma = pltpu.SemaphoreType.DMA
    return pl.pallas_call(
        functools.partial(kernel, (A, R, C, X, hp, H, group)),
        out_shape=pltpu.VMEM((rows, out_columns), bf16),
        in_specs=[pl.BlockSpec(memory_space=pltpu.SMEM)] + [hbm] * 8,
        out_specs=vmem,
        scratch_shapes=[
            pltpu.VMEM((hp, A * rows, HEAD_DIM), bf16),
            pltpu.VMEM((hp, 2, R * C, A * rows, HEAD_DIM), bf16),
            pltpu.VMEM((R * C, A, pad, hp * HEAD_DIM), bf16),
            pltpu.VMEM((hp, 2, text, HEAD_DIM), bf16),
            pltpu.VMEM((hp, A * rows, HEAD_DIM), bf16),
            pltpu.VMEM((hp, rows, X * A * HEAD_DIM), bf16),
            pltpu.VMEM((hp, X * A * HEAD_DIM, out_columns), bf16),
            pltpu.VMEM((rows, out_columns), jnp.float32),
            pltpu.VMEM(pick.shape, bf16),
            pltpu.VMEM((A * rows, R * C * A * rows), jnp.float32),
            pltpu.VMEM(text_keys.shape, bf16),
            pltpu.VMEM(text_values.shape, bf16),
            pltpu.VMEM((1, text), jnp.int32),
            pltpu.VMEM((pad, columns), jnp.float32),
            pltpu.VMEM((pad, columns), bf16),
            pltpu.VMEM((pad, columns), bf16),
            dma,
            dma((4,)),
            dma,
            dma,
            dma((hp, H + 1)),
            dma,
            dma,
            dma,
            dma((hp - 1 + H,)),
            dma,
            dma((hp, H, shares)),
            dma,
            dma((shares,)),
        ],
        compiler_params=pltpu.CompilerParams(
            collective_id=0, has_side_effects=True, vmem_limit_bytes=60 * 1024 * 1024
        ),
    )(text_length, queries, keys, values, text_keys, text_values, jnp.asarray(order), pick, out_weight)


def solution(mesh):
    sizes = (mesh.shape["seq"], mesh.shape["head"], mesh.shape["section"])
    tokens = P(("groups", "seq", "head"), "section")
    return jax.shard_map(
        functools.partial(shards, sizes),
        mesh=mesh,
        in_specs=(tokens,) * 5 + (P("groups"), P(None, "section")),
        out_specs=tokens,
        check_vma=False,
    )
```

```python
import functools
import math

import jax
import jax.numpy as jnp
import numpy as np
from jax import lax
from jax.experimental import pallas as pl
from jax.experimental.pallas import tpu as pltpu
from jax.sharding import PartitionSpec as P

HEAD_DIM = 128
MESH = pl.DeviceIdType.MESH


def kernel(
    dims,
    length_ref,
    q_ref,
    k_ref,
    v_ref,
    tk_hbm,
    tv_hbm,
    order_hbm,
    pick_hbm,
    w_hbm,
    o_ref,
    qb,
    kv,
    tb,
    tkv,
    ob,
    att,
    wb,
    acc,
    pick_ref,
    scores,
    tk_ref,
    tv_ref,
    order_ref,
    wide,
    packed,
    t_ref,
    local_sem,
    early_sem,
    w_sem,
    x_send,
    x_recv,
    t_send,
    t_recv,
    o_send,
    o_recv,
    kv2_send,
    kv2_recv,
    t2_send,
    t2_recv,
):
    A, R, C, X, hp, H, group = dims
    d = HEAD_DIM
    rows = q_ref.shape[0]
    HB, G = A // H, A // group
    seq = lax.axis_index("seq")
    core = lax.axis_index("head")
    section = lax.axis_index("section")
    a = seq // R
    r = lax.rem(seq, R)
    slot = r * C + core
    width = hp * d
    own_half = a // HB
    halves = [lax.rem(own_half + h, H) for h in range(H)]

    def at(a2=None, r2=None, c2=None, x2=None):
        return {
            "seq": (a if a2 is None else a2) * R + (r if r2 is None else r2),
            "head": core if c2 is None else c2,
            "section": section if x2 is None else x2,
        }

    def cols(start, size):
        return pl.ds(pl.multiple_of(start, d), size)

    def own_rows(which):
        return pl.ds(pl.multiple_of(which * rows, 16), rows)

    def half_rows(h):
        return pl.ds(pl.multiple_of(h * HB * rows, 16), HB * rows)

    barrier = pltpu.get_barrier_semaphore()

    def greet(target):
        pl.semaphore_signal(barrier, inc=1, device_id=target, device_id_type=MESH)

    for da in range(A):
        for dx in range(X):
            if da or dx:
                greet(at(a2=lax.rem(a + da, A), x2=lax.rem(section + dx, X)))
    for dr in range(1, R):
        greet(at(r2=lax.rem(r + dr, R)))
    for dc in range(1, C):
        greet(at(c2=lax.rem(core + dc, C)))

    def remote(src, dst, send, recv, target):
        return pltpu.make_async_remote_copy(
            src_ref=src, dst_ref=dst, send_sem=send, recv_sem=recv, device_id=target, device_id_type=MESH
        )

    def drain(ref, sem):
        pltpu.make_async_copy(ref, ref, sem).wait()

    def landing(j, n):
        return qb.at[j] if n == 2 else kv.at[j, n, slot]

    def first(j, n, a2):
        src = (k_ref, v_ref, q_ref)[n].at[:, cols((a2 * hp + j) * d, d)]
        remote(src, landing(j, n).at[own_rows(a)], x_send, x_recv.at[j, H if n == 2 else own_half], at(a2=a2)).start()

    def first_own(j, n):
        src = (k_ref, v_ref, q_ref)[n].at[:, cols((a * hp + j) * d, d)]
        pltpu.make_async_copy(src, landing(j, n).at[own_rows(a)], x_recv.at[j, H if n == 2 else own_half]).start()

    def first_text(a2):
        remote(t_ref.at[:, cols(a2 * width, width)], tb.at[slot, a], t_send, t_recv, at(a2=a2)).start()

    staged = [(tk_hbm, tk_ref), (tv_hbm, tv_ref), (order_hbm, order_ref), (pick_hbm, pick_ref)]
    staged = [pltpu.make_async_copy(src, dst, early_sem.at[i]) for i, (src, dst) in enumerate(staged)]
    for copy in staged:
        copy.start()
    for copy in staged:
        copy.wait()
    count = tk_ref.shape[0]
    if 2 * count < wide.shape[0]:
        wide[...] = jnp.zeros_like(wide)
    wide[:count] = tk_ref[...].astype(jnp.float32)
    wide[count : 2 * count] = tv_ref[...].astype(jnp.float32)
    packed[...] = wide[...].astype(jnp.bfloat16)
    text_copy = pltpu.make_async_copy(packed, t_ref, local_sem)
    text_copy.start()
    for n in range(3):
        first_own(0, n)

    pl.semaphore_wait(barrier, A * X - 1 + R - 1 + C - 1)

    def send_all(j, which):
        for n in which:
            for da in range(1, A):
                first(j, n, lax.rem(a + da, A))
            if j > 0:
                first_own(j, n)

    text_copy.wait()
    pltpu.make_async_copy(t_ref.at[:, cols(a * width, width)], tb.at[slot, a], t_recv).start()
    for da in range(1, A):
        first_text(lax.rem(a + da, A))

    send_all(0, (0, 1))
    for j in range(hp):
        if j + 1 < hp:
            send_all(j + 1, (0, 1))
        send_all(j, (2,))

    for j in range(hp):
        for b in range(X * A):
            pltpu.make_async_copy(
                w_hbm.at[pl.ds((b * hp + j) * d, d)], wb.at[j, pl.ds(b * d, d)], w_sem
            ).start()

    def members():
        for dr in range(1, R):
            yield dr - 1, at(r2=lax.rem(r + dr, R))
        for dc in range(1, C):
            yield R - 2 + dc, at(c2=lax.rem(core + dc, C))

    def share(block, send, recv):
        for n, target in members():
            remote(block(slot), block(slot), send, recv.at[n], target).start()

    def forward(block, send, recv):
        base = R - 1 + C - 1
        for dr in range(1, R):
            from_slot = lax.rem(r - dr + R, R) * C + core
            drain(block(from_slot), recv.at[dr - 1])
            for dc in range(1, C):
                n = base + (dr - 1) * (C - 1) + dc - 1
                remote(
                    block(from_slot), block(from_slot), send, recv.at[n], at(c2=lax.rem(core + dc, C))
                ).start()

    def collect(block, recv):
        base = R - 1 + C - 1
        for dc in range(1, C):
            from_core = lax.rem(core - dc + C, C)
            drain(block(r * C + from_core), recv.at[R - 2 + dc])
            for dr in range(1, R):
                n = base + (dr - 1) * (C - 1) + dc - 1
                drain(block(lax.rem(r - dr + R, R) * C + from_core), recv.at[n])

    def kv_block(j, h):
        return lambda s: kv.at[j, :, s, half_rows(h)]

    def text_block(s):
        return tb.at[s]

    def share_kv(j, h):
        drain(kv.at[j, :, slot, half_rows(h)], x_recv.at[j, h])
        share(kv_block(j, h), kv2_send, kv2_recv.at[j, h])

    def forward_kv(j, h):
        forward(kv_block(j, h), kv2_send, kv2_recv.at[j, h])

    def collect_kv(j):
        for h in halves:
            collect(kv_block(j, h), kv2_recv.at[j, h])

    def wait_q(j):
        drain(qb.at[j], x_recv.at[j, H])

    def project(j, parts, first_term, last_term):
        columns = o_ref.shape[1]
        step = 1536 if columns % 1536 == 0 else d
        if parts is None:
            drain(att.at[j], o_recv.at[j])
            pieces = [pl.ds(0, X * A * d)]
        else:
            for h in parts:
                drain(att.at[j, :, pl.ds(0, X * HB * d)], o_recv.at[j + h])
            pieces = [cols((x * A + h * HB) * d, HB * d) for h in parts for x in range(X)]

        @pl.loop(0, columns // step)
        def _(i):
            part = pl.ds(pl.multiple_of(i * step, d), step)
            term = None if first_term else acc[:, part]
            for piece in pieces:
                got = jnp.dot(att[j, :, piece], wb[j, piece, part], preferred_element_type=jnp.float32)
                term = got if term is None else term + got
            if last_term:
                o_ref[:, part] = term.astype(o_ref.dtype)
            else:
                acc[:, part] = term

    scale = math.log2(math.e) * d ** (-0.5)
    nt = (((1,), (1,)), ((), ()))
    total_keys = R * C * A * rows
    span = next((n for n in (1280, 512, 256, 128) if total_keys % n == 0), total_keys)

    def lanes(x, combine, start):
        for c in range(0, x.shape[1], d):
            start = combine(start, x[:, c : c + d])
        return start

    def flat(j, n, s):
        return kv[j, n].reshape(-1, d)[s * span : (s + 1) * span]

    def attend(j):
        q = qb[j]
        text_scores = lax.dot_general(q, tkv[j, 0], nt, preferred_element_type=jnp.float32)
        text_scores = jnp.where(order_ref[...] < length_ref[0], text_scores, -1e30)
        top = lanes(text_scores[:, d:], jnp.maximum, text_scores[:, :d])
        for s in range(total_keys // span):
            part = lax.dot_general(q, flat(j, 0, s), nt, preferred_element_type=jnp.float32)
            scores[:, s * span : (s + 1) * span] = part
            top = lanes(part, jnp.maximum, top)
        top = jnp.max(top, axis=1, keepdims=True)
        p = jnp.exp2((text_scores - top) * scale)
        total = lanes(p[:, d:], jnp.add, p[:, :d])
        o = jnp.dot(p.astype(jnp.bfloat16), tkv[j, 1], preferred_element_type=jnp.float32)
        for s in range(total_keys // span):
            p = jnp.exp2((scores[:, s * span : (s + 1) * span] - top) * scale)
            total = lanes(p, jnp.add, total)
            o = o + jnp.dot(p.astype(jnp.bfloat16), flat(j, 1, s), preferred_element_type=jnp.float32)
        total = jnp.sum(total, axis=1, keepdims=True)
        ob[j] = (o / total).astype(jnp.bfloat16)

    column = cols((section * A + a) * d, d)
    own = a // group

    def back(j, a2, dx):
        remote(
            ob.at[j, own_rows(a2)],
            att.at[j, :, column],
            o_send,
            o_recv.at[j + own_half if j == hp - 1 else j],
            at(a2=a2, x2=lax.rem(section + dx, X)),
        ).start()

    def back_group(j, i):
        for b in range(group):
            a2 = i * group + b
            for dx in range(1, X):
                back(j, a2, dx)

            @pl.when(a2 != a)
            def _():
                back(j, a2, 0)

            @pl.when(a2 == a)
            def _():
                pltpu.make_async_copy(ob.at[j, own_rows(a2)], att.at[j, :, column], o_recv.at[j + own_half if j == hp - 1 else j]).start()

    def attention(j):
        attend(j)

        @pl.loop(0, G)
        def _(k):
            back_group(j, lax.rem(own + 1 + k, G))

    drain(tb.at[slot], t_recv)
    share(text_block, t2_send, t2_recv)
    for h in halves:
        share_kv(0, h)
    forward(text_block, t2_send, t2_recv)
    if hp > 1:
        for h in halves:
            share_kv(1, h)
    for h in halves:
        forward_kv(0, h)
    collect(text_block, t2_recv)
    block = tb[...].reshape(-1, width)
    for n in range(2):
        got = jnp.dot(pick_ref[n], block, preferred_element_type=jnp.float32).astype(jnp.bfloat16)
        for i in range(hp):
            tkv[i, n] = got[:, i * d : (i + 1) * d]
    for j in range(hp):
        if j + 2 < hp:
            share_kv(j + 2, halves[0])
        wait_q(j)
        collect_kv(j)
        attention(j)
        if j + 1 < hp:
            for h in halves:
                forward_kv(j + 1, h)
        if j + 2 < hp:
            for h in halves[1:]:
                share_kv(j + 2, h)
    drain(wb, w_sem)
    for j in range(hp - 1):
        project(j, None, j == 0, False)
    others = R * C - 1
    if others:
        drain(kv.at[:, :, pl.ds(0, others)], kv2_send)
        drain(tb.at[pl.ds(0, others)], t2_send)
    if A > 1:
        for n in range(3):
            drain(qb.at[:, pl.ds(0, (A - 1) * rows)], x_send)
        drain(tb.at[slot, pl.ds(0, A - 1)], t_send)
    for k, h in enumerate(halves):
        project(hp - 1, [h], hp == 1 and k == 0, k == H - 1)
    if A * X > 1:
        drain(att.at[:, :, pl.ds(0, (A * X - 1) * d)], o_send)


def shards(sizes, queries, keys, values, text_keys, text_values, text_length, out_weight):
    S, C, X = sizes
    rows, columns = queries.shape
    heads = columns // HEAD_DIM
    A = math.gcd(heads, S)
    R = S // A
    hp = heads // A
    text_rows = text_keys.shape[0]
    text = text_rows * S * C
    bf16 = jnp.bfloat16
    pad = -(-2 * text_rows // 8) * 8
    t = np.arange(text)
    block, i = t // text_rows, t % text_rows
    from_slot, from_a = block // A, block % A
    from_r, from_c = from_slot // C, from_slot % C
    order = (((from_a * R + from_r) * C + from_c) * text_rows + i).astype(np.int32)[None, :]
    pick = np.zeros((2, text, R * C * A * pad), np.float32)
    for n in range(2):
        pick[n, t, block * pad + n * text_rows + i] = 1.0
    pick = jnp.asarray(pick, bf16)
    out_columns = out_weight.shape[1]
    shares = R - 1 + C - 1 + (R - 1) * (C - 1)
    H = group = 2 if A % 2 == 0 else 1
    vmem = pl.BlockSpec(memory_space=pltpu.VMEM)
    hbm = pl.BlockSpec(memory_space=pl.ANY)
    dma = pltpu.SemaphoreType.DMA
    return pl.pallas_call(
        functools.partial(kernel, (A, R, C, X, hp, H, group)),
        out_shape=pltpu.VMEM((rows, out_columns), bf16),
        in_specs=[pl.BlockSpec(memory_space=pltpu.SMEM)] + [hbm] * 8,
        out_specs=vmem,
        scratch_shapes=[
            pltpu.VMEM((hp, A * rows, HEAD_DIM), bf16),
            pltpu.VMEM((hp, 2, R * C, A * rows, HEAD_DIM), bf16),
            pltpu.VMEM((R * C, A, pad, hp * HEAD_DIM), bf16),
            pltpu.VMEM((hp, 2, text, HEAD_DIM), bf16),
            pltpu.VMEM((hp, A * rows, HEAD_DIM), bf16),
            pltpu.VMEM((hp, rows, X * A * HEAD_DIM), bf16),
            pltpu.VMEM((hp, X * A * HEAD_DIM, out_columns), bf16),
            pltpu.VMEM((rows, out_columns), jnp.float32),
            pltpu.VMEM(pick.shape, bf16),
            pltpu.VMEM((A * rows, R * C * A * rows), jnp.float32),
            pltpu.VMEM(text_keys.shape, bf16),
            pltpu.VMEM(text_values.shape, bf16),
            pltpu.VMEM((1, text), jnp.int32),
            pltpu.VMEM((pad, columns), jnp.float32),
            pltpu.VMEM((pad, columns), bf16),
            pltpu.VMEM((pad, columns), bf16),
            dma,
            dma((4,)),
            dma,
            dma,
            dma((hp, H + 1)),
            dma,
            dma,
            dma,
            dma((hp - 1 + H,)),
            dma,
            dma((hp, H, shares)),
            dma,
            dma((shares,)),
        ],
        compiler_params=pltpu.CompilerParams(
            collective_id=0, has_side_effects=True, vmem_limit_bytes=60 * 1024 * 1024
        ),
    )(text_length, queries, keys, values, text_keys, text_values, jnp.asarray(order), pick, out_weight)


def solution(mesh):
    sizes = (mesh.shape["seq"], mesh.shape["head"], mesh.shape["section"])
    tokens = P(("groups", "seq", "head"), "section")
    return jax.shard_map(
        functools.partial(shards, sizes),
        mesh=mesh,
        in_specs=(tokens,) * 5 + (P("groups"), P(None, "section")),
        out_specs=tokens,
        check_vma=False,
    )
```
